32 devices in a mesh: space: 8 (over y, x, core), chan: 4 (over z).
Axes of the slice: x: 2, y: 2, z: 4, core: 2. Of those that a mesh axis runs over, the one named last changes fastest.
Arguments:
- feats: bfloat16 [96, 8, 8, 128], P('chan', 'space'), may hold values from -6 to 6
- grads: bfloat16 [96, 8, 8, 128], P('chan', 'space'), may hold values from -6 to 6
- mask: int32 [8, 8, 128], P('space', None, 'chan'), may hold values 0 or 1
- w_first: bfloat16 [27, 96, 96], replicated, may hold values from -0.125 to 0.125
- w_second: bfloat16 [27, 96, 96], replicated, may hold values from -0.125 to 0.125
Outputs:
- grad_feats: bfloat16 [96, 8, 8, 128], P('chan', 'space')
- grad_first: float32 [27, 96, 96], P(None, None, 'chan')
- grad_second: float32 [27, 96, 96], P(None, None, 'chan')
The draws below stay inside these ranges and needn't reach their ends.
All inputs are finite; a program needn't handle non-finite values. No bound on the sum of `mask` on one device may be relied on, other than what follows from the above.
Results may differ from the reference program's by a relative error of at most 0.02.
Values may be sent and summed in bfloat16 or wider, within the bound.
A program may use at most 64 MiB of HBM per device.

```python
import jax
import jax.numpy as jnp

C = 96
TAPS = 27
SY = 8
NX = 8
NZ = 128


def with_ends(drawn, key, low, top_value):
    dims = drawn.shape
    spot = [jax.random.randint(jax.random.fold_in(key, axis), (), 0, dims[axis]) for axis in range(len(dims))]
    drawn = drawn.at[tuple(spot)].set(low)
    longest = dims.index(max(dims))
    spot[longest] = (spot[longest] + 1) % dims[longest]
    return drawn.at[tuple(spot)].set(top_value)


def with_spikes(values, rng, source, target, parts, factor):
    def block_of(position):
        return (jnp.arange(values.shape[position]) // (values.shape[position] // parts)).reshape((-1,) + (1,) * (values.ndim - 1 - position))

    first = jax.random.permutation(rng, parts)[block_of(target)]
    second = (block_of(target) + parts // 2) % parts
    return jnp.where((block_of(source) == first) | (block_of(source) == second), factor * values, values)


def levels(stream_key, dims, split, least, high):
    loudness, own = 1.0, jax.random.fold_in(stream_key, 6)
    for position, parts in split:
        draws = jnp.exp(jax.random.uniform(jax.random.fold_in(own, position), (parts,), jnp.float32, least / len(split), high / len(split)))
        loudness = loudness * jnp.repeat(draws, dims[position] // parts).reshape([-1 if axis == position else 1 for axis in range(len(dims))])
    return loudness


def normal_values(rng, dims, deviation, bound, split=(), dtype=jnp.bfloat16):
    drawn = jax.random.normal(rng, dims, jnp.float32) * deviation
    if len(split) > 0:
        drawn = levels(rng, dims, split, -0.22, 0.18) * drawn
    return jnp.clip(drawn, min=-bound, max=bound).astype(dtype)


def noise_with(stream_key, shape, spread, reach, pieces, heavy, held_as=jnp.bfloat16):
    drawn = spread * jax.random.normal(stream_key, shape, jnp.float32)
    if pieces:
        drawn = drawn * levels(stream_key, shape, pieces, -0.22, 0.18)
    return jnp.clip(with_spikes(drawn, jax.random.fold_in(stream_key, 3), *heavy), -reach, reach).astype(held_as)


def setup_inputs(seed: int = 0) -> dict:
    splits = jax.random.split(jax.random.key(seed), 6)
    return {
        "feats": normal_values(splits[0], (C, NX, SY, NZ), 1.0, 6.0, ((0, 4), (1, 8))),
        "grads": noise_with(splits[1], (C, NX, SY, NZ), 1.0, 6.0, ((0, 4), (1, 8)), (1, 0, 8, 2.0)),
        "mask": with_ends((jax.random.randint(splits[2], (NX, SY, NZ), 0, 4) < 3).astype(jnp.int32), jax.random.fold_in(splits[2], 1), 0, 1),
        "w_first": normal_values(splits[3], (TAPS, C, C), (TAPS * C) ** -0.5, 0.125),
        "w_second": normal_values(splits[4], (TAPS, C, C), (TAPS * C) ** -0.5, 0.125),
    }


offset_table = [(a, b, c) for a in (-1, 0, 1) for b in (-1, 0, 1) for c in (-1, 0, 1)]

def padded_field(field):
    return jnp.pad(field, ((0, 0), (1, 1), (1, 1), (1, 1)))

def shifted(padded, a, b, c):
    channels, xs, ys, zs = padded.shape
    piece = padded[:, 1 + a:xs - 1 + a, 1 + b:ys - 1 + b, 1 + c:zs - 1 + c]
    return piece.reshape(channels, -1)

def reference(feats, grads, mask, w_first, w_second):
    channels, xs, ys, zs = feats.shape
    cells = xs * ys * zs
    weight_mask = mask.astype(jnp.float32).reshape(1, cells)
    padded_x = padded_field(feats)
    pre = jnp.zeros((channels, cells), jnp.float32)
    for k, (a, b, c) in enumerate(offset_table):
        pre = pre + jnp.dot(w_first[k].T, shifted(padded_x, a, b, c), preferred_element_type=jnp.float32)
    pre = pre * weight_mask
    sigm = jax.nn.sigmoid(pre)
    active = (pre * sigm).astype(jnp.bfloat16)
    masked = grads * mask.astype(jnp.bfloat16)[None]
    padded_g = padded_field(masked)
    back = jnp.zeros((channels, cells), jnp.float32)
    seconds = []
    for k, (a, b, c) in enumerate(offset_table):
        moved = shifted(padded_g, -a, -b, -c)
        back = back + jnp.dot(w_second[k], moved, preferred_element_type=jnp.float32)
        seconds.append(jnp.dot(active, moved.T, preferred_element_type=jnp.float32))
    slope = sigm * (1.0 + pre * (1.0 - sigm))
    grad_pre = (back * slope * weight_mask).astype(jnp.bfloat16)
    padded_h = padded_field(grad_pre.reshape(channels, xs, ys, zs))
    grad_in = jnp.zeros((channels, cells), jnp.float32)
    firsts = []
    for k, (a, b, c) in enumerate(offset_table):
        grad_in = grad_in + jnp.dot(w_first[k], shifted(padded_h, -a, -b, -c), preferred_element_type=jnp.float32)
        firsts.append(jnp.dot(shifted(padded_x, a, b, c), grad_pre.T, preferred_element_type=jnp.float32))
    grad_feats = (grad_in * weight_mask).astype(jnp.bfloat16).reshape(channels, xs, ys, zs)
    scale = 1.0 / jnp.sqrt(jnp.float32(cells))
    grad_first = jnp.stack(firsts) * scale
    grad_second = jnp.stack(seconds) * scale
    return (grad_feats, grad_first, grad_second)
```

```python
import functools

import jax
import jax.numpy as jnp
from jax import lax
from jax.experimental import pallas as pl
from jax.experimental.pallas import tpu as pltpu
from jax.sharding import PartitionSpec as P

MESH = pl.DeviceIdType.MESH
F32 = jnp.float32
BF16 = jnp.bfloat16


def dot_nn(left, right):
    return jnp.dot(left, right, preferred_element_type=F32)


def dot_nt(left, right):
    return lax.dot_general(left, right, (((1,), (1,)), ((), ())), preferred_element_type=F32)


def one_hot(rows, cols, target):
    r = lax.broadcasted_iota(jnp.int32, (rows, cols), 0)
    q = lax.broadcasted_iota(jnp.int32, (rows, cols), 1)
    return jnp.where(target(r, q), 1.0, 0.0).astype(BF16)


def lane_shift(x, s):
    if s == 0:
        return x
    n = x.shape[1]
    z = lax.broadcasted_iota(jnp.int32, x.shape, 1)
    if s == 1:
        return jnp.where(z < n - 1, pltpu.roll(x, n - 1, 1), 0.0)
    return jnp.where(z > 0, pltpu.roll(x, 1, 1), 0.0)


def tap_sum(p_ref, base, cb, ys, zs, y, direction):
    total = None
    for c in (-1, 0, 1):
        acc = None
        for b in (-1, 0, 1):
            yy = y + direction * b
            if 0 <= yy < ys:
                j = 3 * (b + 1) + (c + 1)
                piece = p_ref[base + j * cb : base + (j + 1) * cb, yy * zs : (yy + 1) * zs]
                acc = piece if acc is None else acc + piece
        acc = lane_shift(acc, direction * c)
        total = acc if total is None else total + acc
    return total


def spread(out_ref, rows_of, cb, ys, zs):
    for y in range(ys):
        row = rows_of(y)
        for c in (-1, 0, 1):
            moved = lane_shift(row, -c)
            for b in (-1, 0, 1):
                j = 3 * (b + 1) + (c + 1)
                if 0 <= y + b < ys:
                    out_ref[j * cb : (j + 1) * cb, (y + b) * zs : (y + b + 1) * zs] = moved
    edge = jnp.zeros((3 * cb, zs), F32)
    out_ref[0 : 3 * cb, (ys - 1) * zs : ys * zs] = edge
    out_ref[6 * cb : 9 * cb, 0:zs] = edge


def kernel(
    n, nz, ys, zs, scale, sp, ch_name,
    block_ref, mask_ref, w1_ref, w2_ref,
    gf_ref, g1_ref, g2_ref,
    B, MK, MX, M, W, WA, WB, WC, WH, PS, SH, SM, C, H, R32, R1, RR1, G1, R2, RR2, G2,
    zs1, zr1, hs1, hr1, ms1, mr1, mhs, mhr, zs2, zr2, hs2, hr2, s1, q1, s2, q2, t1, u1, t2, u2,
):
    s = lax.axis_index(sp)
    me = lax.axis_index(ch_name)
    cb2, cells = block_ref.shape
    cb = cb2 // 2
    full = cb * nz
    hrows = H.shape[2]
    mz = mask_ref.shape[1]
    rows = 27 * cb

    def copy(src, dst, ssem, rsem, ds, dc):
        return pltpu.make_async_remote_copy(
            src_ref=src, dst_ref=dst, send_sem=ssem, recv_sem=rsem,
            device_id=(ds, dc), device_id_type=MESH,
        )

    barrier = pltpu.get_barrier_semaphore()

    @pl.loop(1, nz)
    def _(i):
        pl.semaphore_signal(barrier, inc=1, device_id=(s, lax.rem(me + i, nz)), device_id_type=MESH)

    @pl.loop(1, n)
    def _(i):
        pl.semaphore_signal(barrier, inc=1, device_id=(lax.rem(s + i, n), me), device_id_type=MESH)

    B[1, me] = block_ref[...]
    place = one_hot(mz, zs, lambda r, q: q == r + mz * me)
    MK[me] = dot_nn(mask_ref[...].astype(F32).astype(BF16), place)
    pl.semaphore_wait(barrier, n + nz - 2)

    def z_copy(i, buf, ssem, rsem):
        return copy(buf, buf, ssem.at[i], rsem.at[i], s, lax.rem(me + i, nz))

    order = sorted(range(1, nz), key=lambda i: min(i, nz - i))
    for i in order:
        z_copy(i, MK.at[me], ms1, mr1).start()
    for i in order:
        z_copy(i, B.at[1, me], zs1, zr1).start()

    def halo(c, start):
        src = B.at[1, c]

        @pl.when(s < n - 1)
        def _():
            d = copy(src, B.at[0, c], hs1.at[0, c], hr1.at[0, c], s + 1, me)
            d.start() if start else d.wait_send()

        @pl.when(s > 0)
        def _():
            d = copy(src, B.at[2, c], hs1.at[1, c], hr1.at[1, c], s - 1, me)
            d.start() if start else d.wait_send()

    halo(me, True)

    pick = one_hot(cb, full, lambda r, q: q == r + cb * me)

    @pl.loop(0, 27)
    def _(k):
        w1 = w1_ref[k]
        W[0, k] = dot_nt(pick, w1)
        W[1, k] = dot_nn(pick, w2_ref[k])
        W[2, k] = dot_nn(pick, w1)

    to_first = one_hot(full, nz * cb2, lambda r, q: q == (r // cb) * cb2 + lax.rem(r, cb))
    to_second = one_hot(full, nz * cb2, lambda r, q: q == (r // cb) * cb2 + cb + lax.rem(r, cb))
    to_halo = one_hot(full, nz * hrows, lambda r, q: q == (r // cb) * hrows + lax.rem(r, cb))
    for a in range(3):
        part = W[0, 9 * a : 9 * a + 9].reshape(9 * cb, full).astype(BF16)
        WA[a] = dot_nn(part, to_first).astype(BF16)
        part = W[1, 9 * a : 9 * a + 9].reshape(9 * cb, full).astype(BF16)
        WB[a] = dot_nn(part, to_second).astype(BF16)
    for a in range(3):
        part = W[2, 9 * a : 9 * a + 9].reshape(9 * cb, full).astype(BF16)
        if a == 1:
            WC[...] = dot_nn(part, to_first).astype(BF16)
        else:
            WH[a // 2] = dot_nn(part, to_halo).astype(BF16)

    for i in order:
        c = lax.rem(me + nz - i, nz)
        copy(MK.at[c], MK.at[c], ms1.at[i], mr1.at[i], s, c).wait_recv()
    own_mask = MK[0]
    for c in range(1, nz):
        own_mask = own_mask + MK[c]
    MX[1] = own_mask

    @pl.when(s < n - 1)
    def _():
        copy(MX.at[1], MX.at[0], mhs.at[0], mhr.at[0], s + 1, me).start()

    @pl.when(s > 0)
    def _():
        copy(MX.at[1], MX.at[2], mhs.at[1], mhr.at[1], s - 1, me).start()

    for i in order:
        c = lax.rem(me + nz - i, nz)
        copy(B.at[1, c], B.at[1, c], zs1.at[i], zr1.at[i], s, c).wait_recv()
        halo(c, True)

    is_grad = lax.rem(lax.broadcasted_iota(jnp.int32, (nz * cb2, zs), 0), cb2) >= cb

    def apply_mask(slab):
        for y in range(ys):
            piece = B[slab, :, :, y * zs : (y + 1) * zs].reshape(nz * cb2, zs)
            factor = jnp.where(is_grad, MX[slab, y : y + 1, :], 1.0).astype(BF16)
            M[slab, :, y * zs : (y + 1) * zs] = piece * factor

    def multiply(slab, first):
        a1, a2 = slab, 2 - slab
        x = M[slab]
        if first:
            PS[0] = dot_nn(WA[a1], x)
            PS[1] = dot_nn(WB[a2], x)
        else:
            PS[0] += dot_nn(WA[a1], x)
            PS[1] += dot_nn(WB[a2], x)

    def spread_masked(slab):
        own = B[slab, me].astype(F32)[cb:cb2]
        spread(
            SM.at[2 - slab],
            lambda y: own[:, y * zs : (y + 1) * zs] * MX[slab, y : y + 1, :],
            cb, ys, zs,
        )

    apply_mask(1)
    multiply(1, True)
    spread_masked(1)
    for side, slab, there in ((0, 0, s > 0), (1, 2, s < n - 1)):

        @pl.when(there)
        def _():
            copy(MX.at[slab], MX.at[slab], mhs.at[side], mhr.at[side], s, me).wait_recv()

            @pl.loop(0, nz)
            def _(c):
                copy(B.at[slab, c], B.at[slab, c], hs1.at[side, c], hr1.at[side, c], s, me).wait_recv()

            apply_mask(slab)
            spread_masked(slab)
            multiply(slab, False)

        @pl.when(jnp.logical_not(there))
        def _():
            M[slab] = jnp.zeros(M.shape[1:], BF16)
            SM[2 - slab] = jnp.zeros(SM.shape[1:], F32)

    for y in range(ys):
        at = slice(y * zs, (y + 1) * zs)
        m = MX[1, y : y + 1, :]
        pre = tap_sum(PS.at[0], 0, cb, ys, zs, y, 1) * m
        back = tap_sum(PS.at[1], 0, cb, ys, zs, y, -1)
        sig = jax.nn.sigmoid(pre)
        active = pre * sig
        slope = sig * (1.0 + pre * (1.0 - sig))
        grad_pre = back * slope * m
        C[me, :, at] = jnp.concatenate([grad_pre, active], axis=0).astype(BF16)

    for i in order:
        z_copy(i, C.at[me], zs2, zr2).start()

    def halo2(c, start):
        src = C.at[c, 0:hrows]

        @pl.when(s < n - 1)
        def _():
            d = copy(src, H.at[0, c], hs2.at[0, c], hr2.at[0, c], s + 1, me)
            d.start() if start else d.wait_send()

        @pl.when(s > 0)
        def _():
            d = copy(src, H.at[1, c], hs2.at[1, c], hr2.at[1, c], s - 1, me)
            d.start() if start else d.wait_send()

    halo2(me, True)

    def scatter(R, RR, ssem, rsem):
        @pl.loop(1, n)
        def _(i):
            p = lax.rem(s + i, n)
            copy(R.at[p], RR.at[i], ssem.at[i], rsem.at[i], p, me).start()

    tail = R32.shape[0] - rows
    if tail:
        R32[rows:, :] = jnp.zeros((tail, full), F32)

    own_gp = C[me].astype(F32)[0:cb]
    spread(SH, lambda y: own_gp[:, y * zs : (y + 1) * zs], cb, ys, zs)
    moved = SH[...].astype(BF16)
    for a in range(3):
        wide = (dot_nt(moved, M[a]) * scale).astype(BF16)
        R32[9 * cb * a : 9 * cb * (a + 1), :] = dot_nt(wide, to_first)
    R1[...] = R32[...].astype(BF16).reshape(R1.shape)
    scatter(R1, RR1, s1, q1)

    for i in order:
        c = lax.rem(me + nz - i, nz)
        copy(C.at[c], C.at[c], zs2.at[i], zr2.at[i], s, c).wait_recv()
        halo2(c, True)

    gathered = C[...].reshape(nz * cb2, cells)
    for a in range(3):
        wide = (dot_nt(SM[a].astype(BF16), gathered) * scale).astype(BF16)
        R32[9 * cb * a : 9 * cb * (a + 1), :] = dot_nt(wide, to_second)
    R2[...] = R32[...].astype(BF16).reshape(R2.shape)
    scatter(R2, RR2, s2, q2)

    PS[0] = dot_nn(WC[...], gathered)

    def gather(R, RR, G, ssem, rsem, ts, us):
        @pl.loop(1, n)
        def _(i):
            copy(RR.at[i], RR.at[i], ssem.at[i], rsem.at[i], s, me).wait_recv()

        total = R[s].astype(F32)
        for i in range(1, n):
            total = total + RR[i].astype(F32)
        G[s] = total.astype(BF16)

        @pl.loop(1, n)
        def _(i):
            p = lax.rem(s + i, n)
            copy(G.at[s], G.at[s], ts.at[i], us.at[i], p, me).start()

    gather(R1, RR1, G1, s1, q1, t1, u1)

    for side, there in ((0, s > 0), (1, s < n - 1)):

        @pl.when(there)
        def _():
            @pl.loop(0, nz)
            def _(c):
                copy(H.at[side, c], H.at[side, c], hs2.at[side, c], hr2.at[side, c], s, me).wait_recv()

            PS[0] += dot_nn(WH[1 - side], H[side].reshape(nz * hrows, cells))

    gather(R2, RR2, G2, s2, q2, t2, u2)
    for y in range(ys):
        at = slice(y * zs, (y + 1) * zs)
        grad_in = tap_sum(PS.at[0], 0, cb, ys, zs, y, -1) * MX[1, y : y + 1, :]
        gf_ref[:, at] = grad_in.astype(BF16)

    def finish(G, out_ref, ts, us):
        @pl.loop(1, n)
        def _(i):
            p = lax.rem(s + n - i, n)
            copy(G.at[p], G.at[p], ts.at[i], us.at[i], s, me).wait_recv()

        out_ref[...] = G[...].astype(F32).reshape(R32.shape)[0:rows]

    finish(G1, g1_ref, t1, u1)
    finish(G2, g2_ref, t2, u2)

    for i in order:
        z_copy(i, MK.at[me], ms1, mr1).wait_send()
        z_copy(i, B.at[1, me], zs1, zr1).wait_send()
        z_copy(i, C.at[me], zs2, zr2).wait_send()

    @pl.when(s < n - 1)
    def _():
        copy(MX.at[1], MX.at[0], mhs.at[0], mhr.at[0], s + 1, me).wait_send()

    @pl.when(s > 0)
    def _():
        copy(MX.at[1], MX.at[2], mhs.at[1], mhr.at[1], s - 1, me).wait_send()

    @pl.loop(0, nz)
    def _(c):
        halo(c, False)
        halo2(c, False)

    @pl.loop(1, n)
    def _(i):
        p = lax.rem(s + i, n)
        copy(R1.at[p], RR1.at[i], s1.at[i], q1.at[i], p, me).wait_send()
        copy(R2.at[p], RR2.at[i], s2.at[i], q2.at[i], p, me).wait_send()
        copy(G1.at[s], G1.at[s], t1.at[i], u1.at[i], p, me).wait_send()
        copy(G2.at[s], G2.at[s], t2.at[i], u2.at[i], p, me).wait_send()


def up(value, step):
    return -(-value // step) * step


def body(n, nz, feats, grads, mask, w_first, w_second):
    cb, _, ys, zs = feats.shape
    taps, full, _ = w_first.shape
    cells = ys * zs
    cb2 = 2 * cb
    hrows = up(cb, 16)
    block = jnp.concatenate([feats.reshape(cb, cells), grads.reshape(cb, cells)], axis=0)
    scale = float((n * ys * zs) ** -0.5)
    rows = taps * cb
    piece = up(-(-rows // n), 16)
    vm = pltpu.VMEM
    dma = pltpu.SemaphoreType.DMA
    spec = pl.BlockSpec(memory_space=pltpu.VMEM)
    reduce_bufs = [vm((n, piece, full), BF16)] * 3
    gf, g1, g2 = pl.pallas_call(
        functools.partial(kernel, n, nz, ys, zs, scale, "space", "chan"),
        out_shape=(
            jax.ShapeDtypeStruct((cb, cells), BF16),
            jax.ShapeDtypeStruct((rows, full), F32),
            jax.ShapeDtypeStruct((rows, full), F32),
        ),
        in_specs=[spec] * 4,
        out_specs=(spec,) * 3,
        scratch_shapes=[
            vm((3, nz, cb2, cells), BF16),
            vm((nz, ys, zs), F32),
            vm((3, ys, zs), F32),
            vm((3, nz * cb2, cells), BF16),
            vm((3, taps, cb, full), F32),
            vm((3, 9 * cb, nz * cb2), BF16),
            vm((3, 9 * cb, nz * cb2), BF16),
            vm((9 * cb, nz * cb2), BF16),
            vm((2, 9 * cb, nz * hrows), BF16),
            vm((2, 9 * cb, cells), F32),
            vm((9 * cb, cells), F32),
            vm((3, 9 * cb, cells), F32),
            vm((nz, cb2, cells), BF16),
            vm((2, nz, hrows, cells), BF16),
            vm((n * piece, full), F32),
            *reduce_bufs,
            *reduce_bufs,
            dma((nz,)), dma((nz,)), dma((2, nz)), dma((2, nz)),
            dma((nz,)), dma((nz,)), dma((2,)), dma((2,)),
            dma((nz,)), dma((nz,)), dma((2, nz)), dma((2, nz)),
            dma((n,)), dma((n,)), dma((n,)), dma((n,)),
            dma((n,)), dma((n,)), dma((n,)), dma((n,)),
        ],
        compiler_params=pltpu.CompilerParams(
            collective_id=0, has_side_effects=True, vmem_limit_bytes=48 << 20
        ),
    )(block, mask.reshape(ys, -1), w_first, w_second)
    return (
        gf.reshape(cb, 1, ys, zs),
        g1.reshape(taps, cb, full).transpose(0, 2, 1),
        g2.reshape(taps, cb, full).transpose(0, 2, 1),
    )


def solution(mesh):
    in_specs = (
        P("chan", "space", None, None),
        P("chan", "space", None, None),
        P("space", None, "chan"),
        P(),
        P(),
    )
    out_specs = (P("chan", "space", None, None), P(None, None, "chan"), P(None, None, "chan"))
    sizes = (mesh.shape["space"], mesh.shape["chan"])
    return jax.shard_map(
        functools.partial(body, *sizes),
        mesh=mesh, in_specs=in_specs, out_specs=out_specs, check_vma=False,
    )
```

```python
import functools

import jax
import jax.numpy as jnp
from jax import lax
from jax.experimental import pallas as pl
from jax.experimental.pallas import tpu as pltpu
from jax.sharding import PartitionSpec as P

MESH = pl.DeviceIdType.MESH
F32 = jnp.float32
BF16 = jnp.bfloat16


def dot_nn(left, right):
    return jnp.dot(left, right, preferred_element_type=F32)


def dot_nt(left, right):
    return lax.dot_general(left, right, (((1,), (1,)), ((), ())), preferred_element_type=F32)


def one_hot(rows, cols, target):
    r = lax.broadcasted_iota(jnp.int32, (rows, cols), 0)
    q = lax.broadcasted_iota(jnp.int32, (rows, cols), 1)
    return jnp.where(target(r, q), 1.0, 0.0).astype(BF16)


def lane_shift(x, s):
    if s == 0:
        return x
    n = x.shape[1]
    z = lax.broadcasted_iota(jnp.int32, x.shape, 1)
    if s == 1:
        return jnp.where(z < n - 1, pltpu.roll(x, n - 1, 1), 0.0)
    return jnp.where(z > 0, pltpu.roll(x, 1, 1), 0.0)


def tap_sum(p_ref, base, cb, ys, zs, y, direction):
    total = None
    for c in (-1, 0, 1):
        acc = None
        for b in (-1, 0, 1):
            yy = y + direction * b
            if 0 <= yy < ys:
                j = 3 * (b + 1) + (c + 1)
                piece = p_ref[base + j * cb : base + (j + 1) * cb, yy * zs : (yy + 1) * zs]
                acc = piece if acc is None else acc + piece
        acc = lane_shift(acc, direction * c)
        total = acc if total is None else total + acc
    return total


def spread(out_ref, rows_of, cb, ys, zs):
    for y in range(ys):
        row = rows_of(y)
        for c in (-1, 0, 1):
            moved = lane_shift(row, -c)
            for b in (-1, 0, 1):
                j = 3 * (b + 1) + (c + 1)
                if 0 <= y + b < ys:
                    out_ref[j * cb : (j + 1) * cb, (y + b) * zs : (y + b + 1) * zs] = moved
    edge = jnp.zeros((3 * cb, zs), F32)
    out_ref[0 : 3 * cb, (ys - 1) * zs : ys * zs] = edge
    out_ref[6 * cb : 9 * cb, 0:zs] = edge


def kernel(
    n, nz, ys, zs, scale, sp, ch_name,
    feats_hbm, grads_hbm, mask_hbm, w1_hbm, w2_hbm,
    gf_ref, g1_ref, g2_ref,
    FI, mask_ref, w1_ref, w2_ref, FX, B, MK, MX, M, W, WA, WB, WH, PS, SH, SM, C, H, R32, R1, RR1, G1, R2, RR2, G2,
    ins, zs1, zf1, zr1, hs1, hr1, ms1, mr1, mhs, mhr, zs2, zf2, zr2, zs3, zf3, zr3, hs2, hr2, s1, q1, s2, q2, t1, u1, t2, u2,
):
    s = lax.axis_index(sp)
    me = lax.axis_index(ch_name)
    cb = FI.shape[1]
    cb2 = 2 * cb
    cells = ys * zs
    full = cb * nz
    hrows = H.shape[2]
    mz = mask_ref.shape[2]
    skip = cb2 - hrows
    rows = 27 * cb

    def copy(src, dst, ssem, rsem, ds, dc):
        return pltpu.make_async_remote_copy(
            src_ref=src, dst_ref=dst, send_sem=ssem, recv_sem=rsem,
            device_id=(ds, dc), device_id_type=MESH,
        )

    barrier = pltpu.get_barrier_semaphore()

    @pl.loop(1, nz)
    def _(i):
        pl.semaphore_signal(barrier, inc=1, device_id=(s, lax.rem(me + i, nz)), device_id_type=MESH)

    @pl.loop(1, n)
    def _(i):
        pl.semaphore_signal(barrier, inc=1, device_id=(lax.rem(s + i, n), me), device_id_type=MESH)

    loads = [
        pltpu.make_async_copy(src, dst, ins.at[i])
        for i, (src, dst) in enumerate((
            (mask_hbm, mask_ref), (feats_hbm, FI.at[0]), (grads_hbm, FI.at[1]),
            (w1_hbm, w1_ref), (w2_hbm, w2_ref),
        ))
    ]
    for load in loads:
        load.start()
    for load in loads[:3]:
        load.wait()

    FX[...] = FI[...].astype(F32).reshape(FX.shape)
    for y in range(ys):
        B[1, me, :, y * zs : (y + 1) * zs] = jnp.concatenate(
            [FX[0, :, y, :], FX[1, :, y, :]], axis=0
        ).astype(BF16)
    place = one_hot(mz, zs, lambda r, q: q == r + mz * me)
    MK[me] = dot_nn(mask_ref[0].astype(F32).astype(BF16), place)
    pl.semaphore_wait(barrier, n + nz - 2)

    def z_copy(i, buf, ssem, rsem):
        return copy(buf, buf, ssem.at[i], rsem.at[i], s, lax.rem(me + i, nz))

    order = sorted(range(1, nz), key=lambda i: min(i, nz - i))
    for i in order:
        z_copy(i, MK.at[me], ms1, mr1).start()

    def inside(c):
        return jnp.logical_and(c >= 0, c < nz)

    def z_own(view, ssem, rsem, start):
        def go(d, there):
            @pl.when(there)
            def _():
                x = copy(view(me), view(me), ssem.at[d + 2], rsem.at[me], s, me + d)
                x.start() if start else x.wait_send()

        relayed = [inside(me + 3 * sign) for sign in (1, -1)]
        for sign in (1, -1):
            if nz > 3:
                go(2 * sign, relayed[sign < 0])
        for sign in (1, -1):
            go(sign, inside(me + sign))
        for sign in (1, -1):
            if nz > 2:
                go(2 * sign, jnp.logical_and(inside(me + 2 * sign), jnp.logical_not(relayed[sign < 0])))

    def z_rest(view, fsem, rsem, after):
        for e in range(1, nz):
            for sign in (1, -1):
                c = me - sign * e

                @pl.when(inside(c))
                def _():
                    if after is not None:
                        copy(view(c), view(c), fsem.at[c], rsem.at[c], s, me).wait_recv()
                    if e >= 2:

                        @pl.when(inside(me + sign))
                        def _():
                            x = copy(view(c), view(c), fsem.at[c], rsem.at[c], s, me + sign)
                            x.start() if after is not None else x.wait_send()

                    if after is not None:
                        after(c)

    def view1(c):
        return B.at[1, c]

    z_own(view1, zs1, zr1, True)

    def halo(c, start):
        src = B.at[1, c]

        @pl.when(s < n - 1)
        def _():
            d = copy(src, B.at[0, c], hs1.at[0, c], hr1.at[0, c], s + 1, me)
            d.start() if start else d.wait_send()

        @pl.when(s > 0)
        def _():
            d = copy(src, B.at[2, c], hs1.at[1, c], hr1.at[1, c], s - 1, me)
            d.start() if start else d.wait_send()

    halo(me, True)

    for load in loads[3:]:
        load.wait()
    pick = one_hot(cb, full, lambda r, q: q == r + cb * me)

    @pl.loop(0, 27)
    def _(k):
        w1 = w1_ref[k]
        W[0, k] = dot_nt(pick, w1)
        W[1, k] = dot_nn(pick, w2_ref[k])
        W[2, k] = dot_nn(pick, w1)

    to_first = one_hot(full, nz * cb2, lambda r, q: q == (r // cb) * cb2 + lax.rem(r, cb))
    to_second = one_hot(full, nz * cb2, lambda r, q: q == (r // cb) * cb2 + cb + lax.rem(r, cb))
    to_halo = one_hot(full, nz * hrows, lambda r, q: q == (r // cb) * hrows + (hrows - cb) + lax.rem(r, cb))
    to_active = one_hot(full, nz * hrows, lambda r, q: q == (r // cb) * hrows + lax.rem(r, cb))
    for a in range(3):
        part = W[0, 9 * a : 9 * a + 9].reshape(9 * cb, full).astype(BF16)
        WA[a] = dot_nn(part, to_first).astype(BF16)
        part = W[1, 9 * a : 9 * a + 9].reshape(9 * cb, full).astype(BF16)
        WB[a] = dot_nn(part, to_second).astype(BF16)
    for a in range(3):
        part = W[2, 9 * a : 9 * a + 9].reshape(9 * cb, full).astype(BF16)
        WH[a] = dot_nn(part, to_halo).astype(BF16)

    for i in order:
        c = lax.rem(me + nz - i, nz)
        copy(MK.at[c], MK.at[c], ms1.at[i], mr1.at[i], s, c).wait_recv()
    own_mask = MK[0]
    for c in range(1, nz):
        own_mask = own_mask + MK[c]
    MX[1] = own_mask

    @pl.when(s < n - 1)
    def _():
        copy(MX.at[1], MX.at[0], mhs.at[0], mhr.at[0], s + 1, me).start()

    @pl.when(s > 0)
    def _():
        copy(MX.at[1], MX.at[2], mhs.at[1], mhr.at[1], s - 1, me).start()

    z_rest(view1, zf1, zr1, lambda c: halo(c, True))

    is_grad = lax.rem(lax.broadcasted_iota(jnp.int32, (nz * cb2, zs), 0), cb2) >= cb

    def apply_mask(slab):
        for y in range(ys):
            piece = B[slab, :, :, y * zs : (y + 1) * zs].reshape(nz * cb2, zs)
            factor = jnp.where(is_grad, MX[slab, y : y + 1, :], 1.0).astype(BF16)
            M[slab, :, y * zs : (y + 1) * zs] = piece * factor

    def multiply(slab, first):
        a1, a2 = slab, 2 - slab
        x = M[slab]
        if first:
            PS[0] = dot_nn(WA[a1], x)
            PS[1] = dot_nn(WB[a2], x)
        else:
            PS[0] += dot_nn(WA[a1], x)
            PS[1] += dot_nn(WB[a2], x)

    def spread_masked(slab):
        own = B[slab, me].astype(F32)[cb:cb2]
        spread(
            SM.at[2 - slab],
            lambda y: own[:, y * zs : (y + 1) * zs] * MX[slab, y : y + 1, :],
            cb, ys, zs,
        )

    apply_mask(1)
    multiply(1, True)
    spread_masked(1)
    for side, slab, there in ((0, 0, s > 0), (1, 2, s < n - 1)):

        @pl.when(there)
        def _():
            copy(MX.at[slab], MX.at[slab], mhs.at[side], mhr.at[side], s, me).wait_recv()

            @pl.loop(0, nz)
            def _(c):
                copy(B.at[slab, c], B.at[slab, c], hs1.at[side, c], hr1.at[side, c], s, me).wait_recv()

            apply_mask(slab)
            spread_masked(slab)
            multiply(slab, False)

        @pl.when(jnp.logical_not(there))
        def _():
            M[slab] = jnp.zeros(M.shape[1:], BF16)
            SM[2 - slab] = jnp.zeros(SM.shape[1:], F32)

    for y in range(ys):
        at = slice(y * zs, (y + 1) * zs)
        m = MX[1, y : y + 1, :]
        pre = tap_sum(PS.at[0], 0, cb, ys, zs, y, 1) * m
        back = tap_sum(PS.at[1], 0, cb, ys, zs, y, -1)
        sig = jax.nn.sigmoid(pre)
        active = pre * sig
        slope = sig * (1.0 + pre * (1.0 - sig))
        grad_pre = back * slope * m
        C[me, :, at] = jnp.concatenate([active, grad_pre], axis=0).astype(BF16)

    def view2(c):
        return C.at[c, 0:hrows]

    def view3(c):
        return C.at[c, hrows:cb2]

    z_own(view2, zs2, zr2, True)
    if skip:
        z_own(view3, zs3, zr3, True)

    def halo2(c, start):
        src = C.at[c, skip:cb2]

        @pl.when(s < n - 1)
        def _():
            d = copy(src, H.at[0, c], hs2.at[0, c], hr2.at[0, c], s + 1, me)
            d.start() if start else d.wait_send()

        @pl.when(s > 0)
        def _():
            d = copy(src, H.at[1, c], hs2.at[1, c], hr2.at[1, c], s - 1, me)
            d.start() if start else d.wait_send()

    halo2(me, True)

    def scatter(R, RR, ssem, rsem):
        @pl.loop(1, n)
        def _(i):
            p = lax.rem(s + i, n)
            copy(R.at[p], RR.at[i], ssem.at[i], rsem.at[i], p, me).start()

    tail = R32.shape[0] - rows
    if tail:
        R32[rows:, :] = jnp.zeros((tail, full), F32)

    own_gp = C[me].astype(F32)[cb:cb2]
    spread(SH, lambda y: own_gp[:, y * zs : (y + 1) * zs], cb, ys, zs)
    moved = SH[...].astype(BF16)
    for a in range(3):
        wide = (dot_nt(moved, M[a]) * scale).astype(BF16)
        R32[9 * cb * a : 9 * cb * (a + 1), :] = dot_nt(wide, to_first)
    R1[...] = R32[...].astype(BF16).reshape(R1.shape)
    scatter(R1, RR1, s1, q1)

    def nothing(c):
        pass

    z_rest(view2, zf2, zr2, nothing if skip else (lambda c: halo2(c, True)))

    gathered = C[:, 0:hrows, :].reshape(nz * hrows, cells)
    for a in range(3):
        wide = (dot_nt(SM[a].astype(BF16), gathered) * scale).astype(BF16)
        R32[9 * cb * a : 9 * cb * (a + 1), :] = dot_nt(wide, to_active)
    R2[...] = R32[...].astype(BF16).reshape(R2.shape)
    scatter(R2, RR2, s2, q2)

    if skip:
        z_rest(view3, zf3, zr3, lambda c: halo2(c, True))
    PS[0] = dot_nn(WH[1], C[:, skip:cb2, :].reshape(nz * hrows, cells))

    def gather(R, RR, G, ssem, rsem, ts, us):
        @pl.loop(1, n)
        def _(i):
            copy(RR.at[i], RR.at[i], ssem.at[i], rsem.at[i], s, me).wait_recv()

        total = R[s].astype(F32)
        for i in range(1, n):
            total = total + RR[i].astype(F32)
        G[s] = total.astype(BF16)

        @pl.loop(1, n)
        def _(i):
            p = lax.rem(s + i, n)
            copy(G.at[s], G.at[s], ts.at[i], us.at[i], p, me).start()

    gather(R1, RR1, G1, s1, q1, t1, u1)

    for side, there in ((0, s > 0), (1, s < n - 1)):

        @pl.when(there)
        def _():
            @pl.loop(0, nz)
            def _(c):
                copy(H.at[side, c], H.at[side, c], hs2.at[side, c], hr2.at[side, c], s, me).wait_recv()

            PS[0] += dot_nn(WH[2 - 2 * side], H[side].reshape(nz * hrows, cells))

    gather(R2, RR2, G2, s2, q2, t2, u2)
    for y in range(ys):
        at = slice(y * zs, (y + 1) * zs)
        grad_in = tap_sum(PS.at[0], 0, cb, ys, zs, y, -1) * MX[1, y : y + 1, :]
        FX[0, :, y, :] = grad_in
    gf_ref[...] = FX[0].astype(BF16).reshape(gf_ref.shape)

    def finish(G, out_ref, ts, us):
        @pl.loop(1, n)
        def _(i):
            p = lax.rem(s + n - i, n)
            copy(G.at[p], G.at[p], ts.at[i], us.at[i], s, me).wait_recv()

        out_ref[...] = G[...].astype(F32).reshape(R32.shape)[0:rows]

    finish(G1, g1_ref, t1, u1)
    finish(G2, g2_ref, t2, u2)

    z_own(view1, zs1, zr1, False)
    z_rest(view1, zf1, zr1, None)
    z_own(view2, zs2, zr2, False)
    z_rest(view2, zf2, zr2, None)
    if skip:
        z_own(view3, zs3, zr3, False)
        z_rest(view3, zf3, zr3, None)
    for i in order:
        z_copy(i, MK.at[me], ms1, mr1).wait_send()

    @pl.when(s < n - 1)
    def _():
        copy(MX.at[1], MX.at[0], mhs.at[0], mhr.at[0], s + 1, me).wait_send()

    @pl.when(s > 0)
    def _():
        copy(MX.at[1], MX.at[2], mhs.at[1], mhr.at[1], s - 1, me).wait_send()

    @pl.loop(0, nz)
    def _(c):
        halo(c, False)
        halo2(c, False)

    @pl.loop(1, n)
    def _(i):
        p = lax.rem(s + i, n)
        copy(R1.at[p], RR1.at[i], s1.at[i], q1.at[i], p, me).wait_send()
        copy(R2.at[p], RR2.at[i], s2.at[i], q2.at[i], p, me).wait_send()
        copy(G1.at[s], G1.at[s], t1.at[i], u1.at[i], p, me).wait_send()
        copy(G2.at[s], G2.at[s], t2.at[i], u2.at[i], p, me).wait_send()


def up(value, step):
    return -(-value // step) * step


def body(n, nz, feats, grads, mask, w_first, w_second):
    cb, _, ys, zs = feats.shape
    taps, full, _ = w_first.shape
    cells = ys * zs
    cb2 = 2 * cb
    hrows = up(cb, 16)
    scale = float((n * ys * zs) ** -0.5)
    rows = taps * cb
    piece = up(-(-rows // n), 16)
    vm = pltpu.VMEM
    dma = pltpu.SemaphoreType.DMA
    spec = pl.BlockSpec(memory_space=pltpu.VMEM)
    reduce_bufs = [vm((n, piece, full), BF16)] * 3
    gf, g1, g2 = pl.pallas_call(
        functools.partial(kernel, n, nz, ys, zs, scale, "space", "chan"),
        out_shape=(
            jax.ShapeDtypeStruct((cb, 1, ys, zs), BF16),
            jax.ShapeDtypeStruct((rows, full), F32),
            jax.ShapeDtypeStruct((rows, full), F32),
        ),
        in_specs=[pl.BlockSpec(memory_space=pltpu.HBM)] * 5,
        out_specs=(spec,) * 3,
        scratch_shapes=[
            vm((2, cb, 1, ys, zs), BF16),
            vm((1, ys, mask.shape[2]), jnp.int32),
            vm((taps, full, full), BF16),
            vm((taps, full, full), BF16),
            vm((2, cb, ys, zs), F32),
            vm((3, nz, cb2, cells), BF16),
            vm((nz, ys, zs), F32),
            vm((3, ys, zs), F32),
            vm((3, nz * cb2, cells), BF16),
            vm((3, taps, cb, full), F32),
            vm((3, 9 * cb, nz * cb2), BF16),
            vm((3, 9 * cb, nz * cb2), BF16),
            vm((3, 9 * cb, nz * hrows), BF16),
            vm((2, 9 * cb, cells), F32),
            vm((9 * cb, cells), F32),
            vm((3, 9 * cb, cells), F32),
            vm((nz, cb2, cells), BF16),
            vm((2, nz, hrows, cells), BF16),
            vm((n * piece, full), F32),
            *reduce_bufs,
            *reduce_bufs,
            dma((5,)), dma((5,)), dma((nz,)), dma((nz,)), dma((2, nz)), dma((2, nz)),
            dma((nz,)), dma((nz,)), dma((2,)), dma((2,)),
            dma((5,)), dma((nz,)), dma((nz,)), dma((5,)), dma((nz,)), dma((nz,)),
            dma((2, nz)), dma((2, nz)),
            dma((n,)), dma((n,)), dma((n,)), dma((n,)),
            dma((n,)), dma((n,)), dma((n,)), dma((n,)),
        ],
        compiler_params=pltpu.CompilerParams(
            collective_id=0, has_side_effects=True, vmem_limit_bytes=48 << 20
        ),
    )(feats, grads, mask, w_first, w_second)
    return (
        gf,
        g1.reshape(taps, cb, full).transpose(0, 2, 1),
        g2.reshape(taps, cb, full).transpose(0, 2, 1),
    )


def solution(mesh):
    in_specs = (
        P("chan", "space", None, None),
        P("chan", "space", None, None),
        P("space", None, "chan"),
        P(),
        P(),
    )
    out_specs = (P("chan", "space", None, None), P(None, None, "chan"), P(None, None, "chan"))
    sizes = (mesh.shape["space"], mesh.shape["chan"])
    return jax.shard_map(
        functools.partial(body, *sizes),
        mesh=mesh, in_specs=in_specs, out_specs=out_specs, check_vma=False,
    )
```

```python
import functools

import jax
import jax.numpy as jnp
from jax import lax
from jax.experimental import pallas as pl
from jax.experimental.pallas import tpu as pltpu
from jax.sharding import PartitionSpec as P

MESH = pl.DeviceIdType.MESH
F32 = jnp.float32
BF16 = jnp.bfloat16


def dot_nn(left, right):
    return jnp.dot(left, right, preferred_element_type=F32)


def dot_nt(left, right):
    return lax.dot_general(left, right, (((1,), (1,)), ((), ())), preferred_element_type=F32)


def one_hot(rows, cols, target):
    r = lax.broadcasted_iota(jnp.int32, (rows, cols), 0)
    q = lax.broadcasted_iota(jnp.int32, (rows, cols), 1)
    return jnp.where(target(r, q), 1.0, 0.0).astype(BF16)


def lane_shift(x, s):
    if s == 0:
        return x
    n = x.shape[1]
    z = lax.broadcasted_iota(jnp.int32, x.shape, 1)
    if s == 1:
        return jnp.where(z < n - 1, pltpu.roll(x, n - 1, 1), 0.0)
    return jnp.where(z > 0, pltpu.roll(x, 1, 1), 0.0)


def tap_sum(p_ref, base, cb, ys, zs, y, direction):
    total = None
    for c in (-1, 0, 1):
        acc = None
        for b in (-1, 0, 1):
            yy = y + direction * b
            if 0 <= yy < ys:
                j = 3 * (b + 1) + (c + 1)
                piece = p_ref[base + j * cb : base + (j + 1) * cb, yy * zs : (yy + 1) * zs]
                acc = piece if acc is None else acc + piece
        acc = lane_shift(acc, direction * c)
        total = acc if total is None else total + acc
    return total


def spread(out_ref, rows_of, cb, ys, zs):
    for y in range(ys):
        row = rows_of(y)
        for c in (-1, 0, 1):
            moved = lane_shift(row, -c)
            for b in (-1, 0, 1):
                j = 3 * (b + 1) + (c + 1)
                if 0 <= y + b < ys:
                    out_ref[j * cb : (j + 1) * cb, (y + b) * zs : (y + b + 1) * zs] = moved
    edge = jnp.zeros((3 * cb, zs), F32)
    out_ref[0 : 3 * cb, (ys - 1) * zs : ys * zs] = edge
    out_ref[6 * cb : 9 * cb, 0:zs] = edge


def kernel(
    n, nz, ys, zs, scale, sp, ch_name,
    block_ref, mask_ref, w1_hbm, w2_hbm,
    gf_ref, g1_ref, g2_ref,
    w1_ref, w2_ref, ws, B, MK, MX, M, W, WA, WB, WC, WH, PS, SH, SM, C, H, R32, R1, RR1, G1, R2, RR2, G2,
    zs1, zr1, hs1, hr1, ms1, mr1, mhs, mhr, zs2, zr2, hs2, hr2, s1, q1, s2, q2, t1, u1, t2, u2,
):
    s = lax.axis_index(sp)
    me = lax.axis_index(ch_name)
    cb2, cells = block_ref.shape
    cb = cb2 // 2
    full = cb * nz
    hrows = H.shape[2]
    mz = mask_ref.shape[1]
    rows = 27 * cb

    def copy(src, dst, ssem, rsem, ds, dc):
        return pltpu.make_async_remote_copy(
            src_ref=src, dst_ref=dst, send_sem=ssem, recv_sem=rsem,
            device_id=(ds, dc), device_id_type=MESH,
        )

    load1 = pltpu.make_async_copy(w1_hbm, w1_ref, ws.at[0])
    load2 = pltpu.make_async_copy(w2_hbm, w2_ref, ws.at[1])
    load1.start()
    load2.start()
    barrier = pltpu.get_barrier_semaphore()

    @pl.loop(1, nz)
    def _(i):
        pl.semaphore_signal(barrier, inc=1, device_id=(s, lax.rem(me + i, nz)), device_id_type=MESH)

    @pl.loop(1, n)
    def _(i):
        pl.semaphore_signal(barrier, inc=1, device_id=(lax.rem(s + i, n), me), device_id_type=MESH)

    B[1, me] = block_ref[...]
    place = one_hot(mz, zs, lambda r, q: q == r + mz * me)
    MK[me] = dot_nn(mask_ref[...].astype(F32).astype(BF16), place)
    pl.semaphore_wait(barrier, n + nz - 2)

    def z_copy(i, buf, ssem, rsem):
        return copy(buf, buf, ssem.at[i], rsem.at[i], s, lax.rem(me + i, nz))

    order = sorted(range(1, nz), key=lambda i: min(i, nz - i))
    for i in order:
        z_copy(i, MK.at[me], ms1, mr1).start()
    for i in order:
        z_copy(i, B.at[1, me], zs1, zr1).start()

    def halo(c, start):
        src = B.at[1, c]

        @pl.when(s < n - 1)
        def _():
            d = copy(src, B.at[0, c], hs1.at[0, c], hr1.at[0, c], s + 1, me)
            d.start() if start else d.wait_send()

        @pl.when(s > 0)
        def _():
            d = copy(src, B.at[2, c], hs1.at[1, c], hr1.at[1, c], s - 1, me)
            d.start() if start else d.wait_send()

    halo(me, True)

    load1.wait()
    load2.wait()
    pick = one_hot(cb, full, lambda r, q: q == r + cb * me)

    @pl.loop(0, 27)
    def _(k):
        w1 = w1_ref[k]
        W[0, k] = dot_nt(pick, w1)
        W[1, k] = dot_nn(pick, w2_ref[k])
        W[2, k] = dot_nn(pick, w1)

    to_first = one_hot(full, nz * cb2, lambda r, q: q == (r // cb) * cb2 + lax.rem(r, cb))
    to_second = one_hot(full, nz * cb2, lambda r, q: q == (r // cb) * cb2 + cb + lax.rem(r, cb))
    to_halo = one_hot(full, nz * hrows, lambda r, q: q == (r // cb) * hrows + lax.rem(r, cb))
    for a in range(3):
        part = W[0, 9 * a : 9 * a + 9].reshape(9 * cb, full).astype(BF16)
        WA[a] = dot_nn(part, to_first).astype(BF16)
        part = W[1, 9 * a : 9 * a + 9].reshape(9 * cb, full).astype(BF16)
        WB[a] = dot_nn(part, to_second).astype(BF16)
    for a in range(3):
        part = W[2, 9 * a : 9 * a + 9].reshape(9 * cb, full).astype(BF16)
        if a == 1:
            WC[...] = dot_nn(part, to_first).astype(BF16)
        else:
            WH[a // 2] = dot_nn(part, to_halo).astype(BF16)

    for i in order:
        c = lax.rem(me + nz - i, nz)
        copy(MK.at[c], MK.at[c], ms1.at[i], mr1.at[i], s, c).wait_recv()
    own_mask = MK[0]
    for c in range(1, nz):
        own_mask = own_mask + MK[c]
    MX[1] = own_mask

    @pl.when(s < n - 1)
    def _():
        copy(MX.at[1], MX.at[0], mhs.at[0], mhr.at[0], s + 1, me).start()

    @pl.when(s > 0)
    def _():
        copy(MX.at[1], MX.at[2], mhs.at[1], mhr.at[1], s - 1, me).start()

    for i in order:
        c = lax.rem(me + nz - i, nz)
        copy(B.at[1, c], B.at[1, c], zs1.at[i], zr1.at[i], s, c).wait_recv()
        halo(c, True)

    is_grad = lax.rem(lax.broadcasted_iota(jnp.int32, (nz * cb2, zs), 0), cb2) >= cb

    def apply_mask(slab):
        for y in range(ys):
            piece = B[slab, :, :, y * zs : (y + 1) * zs].reshape(nz * cb2, zs)
            factor = jnp.where(is_grad, MX[slab, y : y + 1, :], 1.0).astype(BF16)
            M[slab, :, y * zs : (y + 1) * zs] = piece * factor

    def multiply(slab, first):
        a1, a2 = slab, 2 - slab
        x = M[slab]
        if first:
            PS[0] = dot_nn(WA[a1], x)
            PS[1] = dot_nn(WB[a2], x)
        else:
            PS[0] += dot_nn(WA[a1], x)
            PS[1] += dot_nn(WB[a2], x)

    def spread_masked(slab):
        own = B[slab, me].astype(F32)[cb:cb2]
        spread(
            SM.at[2 - slab],
            lambda y: own[:, y * zs : (y + 1) * zs] * MX[slab, y : y + 1, :],
            cb, ys, zs,
        )

    apply_mask(1)
    multiply(1, True)
    spread_masked(1)
    for side, slab, there in ((0, 0, s > 0), (1, 2, s < n - 1)):

        @pl.when(there)
        def _():
            copy(MX.at[slab], MX.at[slab], mhs.at[side], mhr.at[side], s, me).wait_recv()

            @pl.loop(0, nz)
            def _(c):
                copy(B.at[slab, c], B.at[slab, c], hs1.at[side, c], hr1.at[side, c], s, me).wait_recv()

            apply_mask(slab)
            spread_masked(slab)
            multiply(slab, False)

        @pl.when(jnp.logical_not(there))
        def _():
            M[slab] = jnp.zeros(M.shape[1:], BF16)
            SM[2 - slab] = jnp.zeros(SM.shape[1:], F32)

    for y in range(ys):
        at = slice(y * zs, (y + 1) * zs)
        m = MX[1, y : y + 1, :]
        pre = tap_sum(PS.at[0], 0, cb, ys, zs, y, 1) * m
        back = tap_sum(PS.at[1], 0, cb, ys, zs, y, -1)
        sig = jax.nn.sigmoid(pre)
        active = pre * sig
        slope = sig * (1.0 + pre * (1.0 - sig))
        grad_pre = back * slope * m
        C[me, :, at] = jnp.concatenate([grad_pre, active], axis=0).astype(BF16)

    for i in order:
        z_copy(i, C.at[me], zs2, zr2).start()

    def halo2(c, start):
        src = C.at[c, 0:hrows]

        @pl.when(s < n - 1)
        def _():
            d = copy(src, H.at[0, c], hs2.at[0, c], hr2.at[0, c], s + 1, me)
            d.start() if start else d.wait_send()

        @pl.when(s > 0)
        def _():
            d = copy(src, H.at[1, c], hs2.at[1, c], hr2.at[1, c], s - 1, me)
            d.start() if start else d.wait_send()

    halo2(me, True)

    def scatter(R, RR, ssem, rsem):
        @pl.loop(1, n)
        def _(i):
            p = lax.rem(s + i, n)
            copy(R.at[p], RR.at[i], ssem.at[i], rsem.at[i], p, me).start()

    tail = R32.shape[0] - rows
    if tail:
        R32[rows:, :] = jnp.zeros((tail, full), F32)

    own_gp = C[me].astype(F32)[0:cb]
    spread(SH, lambda y: own_gp[:, y * zs : (y + 1) * zs], cb, ys, zs)
    moved = SH[...].astype(BF16)
    for a in range(3):
        wide = (dot_nt(moved, M[a]) * scale).astype(BF16)
        R32[9 * cb * a : 9 * cb * (a + 1), :] = dot_nt(wide, to_first)
    R1[...] = R32[...].astype(BF16).reshape(R1.shape)
    scatter(R1, RR1, s1, q1)

    for i in order:
        c = lax.rem(me + nz - i, nz)
        copy(C.at[c], C.at[c], zs2.at[i], zr2.at[i], s, c).wait_recv()
        halo2(c, True)

    gathered = C[...].reshape(nz * cb2, cells)
    for a in range(3):
        wide = (dot_nt(SM[a].astype(BF16), gathered) * scale).astype(BF16)
        R32[9 * cb * a : 9 * cb * (a + 1), :] = dot_nt(wide, to_second)
    R2[...] = R32[...].astype(BF16).reshape(R2.shape)
    scatter(R2, RR2, s2, q2)

    PS[0] = dot_nn(WC[...], gathered)

    def gather(R, RR, G, ssem, rsem, ts, us):
        @pl.loop(1, n)
        def _(i):
            copy(RR.at[i], RR.at[i], ssem.at[i], rsem.at[i], s, me).wait_recv()

        total = R[s].astype(F32)
        for i in range(1, n):
            total = total + RR[i].astype(F32)
        G[s] = total.astype(BF16)

        @pl.loop(1, n)
        def _(i):
            p = lax.rem(s + i, n)
            copy(G.at[s], G.at[s], ts.at[i], us.at[i], p, me).start()

    gather(R1, RR1, G1, s1, q1, t1, u1)

    for side, there in ((0, s > 0), (1, s < n - 1)):

        @pl.when(there)
        def _():
            @pl.loop(0, nz)
            def _(c):
                copy(H.at[side, c], H.at[side, c], hs2.at[side, c], hr2.at[side, c], s, me).wait_recv()

            PS[0] += dot_nn(WH[1 - side], H[side].reshape(nz * hrows, cells))

    gather(R2, RR2, G2, s2, q2, t2, u2)
    for y in range(ys):
        at = slice(y * zs, (y + 1) * zs)
        grad_in = tap_sum(PS.at[0], 0, cb, ys, zs, y, -1) * MX[1, y : y + 1, :]
        gf_ref[:, at] = grad_in.astype(BF16)

    def finish(G, out_ref, ts, us):
        @pl.loop(1, n)
        def _(i):
            p = lax.rem(s + n - i, n)
            copy(G.at[p], G.at[p], ts.at[i], us.at[i], s, me).wait_recv()

        out_ref[...] = G[...].astype(F32).reshape(R32.shape)[0:rows]

    finish(G1, g1_ref, t1, u1)
    finish(G2, g2_ref, t2, u2)

    for i in order:
        z_copy(i, MK.at[me], ms1, mr1).wait_send()
        z_copy(i, B.at[1, me], zs1, zr1).wait_send()
        z_copy(i, C.at[me], zs2, zr2).wait_send()

    @pl.when(s < n - 1)
    def _():
        copy(MX.at[1], MX.at[0], mhs.at[0], mhr.at[0], s + 1, me).wait_send()

    @pl.when(s > 0)
    def _():
        copy(MX.at[1], MX.at[2], mhs.at[1], mhr.at[1], s - 1, me).wait_send()

    @pl.loop(0, nz)
    def _(c):
        halo(c, False)
        halo2(c, False)

    @pl.loop(1, n)
    def _(i):
        p = lax.rem(s + i, n)
        copy(R1.at[p], RR1.at[i], s1.at[i], q1.at[i], p, me).wait_send()
        copy(R2.at[p], RR2.at[i], s2.at[i], q2.at[i], p, me).wait_send()
        copy(G1.at[s], G1.at[s], t1.at[i], u1.at[i], p, me).wait_send()
        copy(G2.at[s], G2.at[s], t2.at[i], u2.at[i], p, me).wait_send()


def up(value, step):
    return -(-value // step) * step


def body(n, nz, feats, grads, mask, w_first, w_second):
    cb, _, ys, zs = feats.shape
    taps, full, _ = w_first.shape
    cells = ys * zs
    cb2 = 2 * cb
    hrows = up(cb, 16)
    block = jnp.concatenate([feats.reshape(cb, cells), grads.reshape(cb, cells)], axis=0)
    scale = float((n * ys * zs) ** -0.5)
    rows = taps * cb
    piece = up(-(-rows // n), 16)
    vm = pltpu.VMEM
    dma = pltpu.SemaphoreType.DMA
    spec = pl.BlockSpec(memory_space=pltpu.VMEM)
    reduce_bufs = [vm((n, piece, full), BF16)] * 3
    gf, g1, g2 = pl.pallas_call(
        functools.partial(kernel, n, nz, ys, zs, scale, "space", "chan"),
        out_shape=(
            jax.ShapeDtypeStruct((cb, cells), BF16),
            jax.ShapeDtypeStruct((rows, full), F32),
            jax.ShapeDtypeStruct((rows, full), F32),
        ),
        in_specs=[spec] * 2 + [pl.BlockSpec(memory_space=pltpu.HBM)] * 2,
        out_specs=(spec,) * 3,
        scratch_shapes=[
            vm((taps, full, full), BF16), vm((taps, full, full), BF16), dma((2,)),
            vm((3, nz, cb2, cells), BF16),
            vm((nz, ys, zs), F32),
            vm((3, ys, zs), F32),
            vm((3, nz * cb2, cells), BF16),
            vm((3, taps, cb, full), F32),
            vm((3, 9 * cb, nz * cb2), BF16),
            vm((3, 9 * cb, nz * cb2), BF16),
            vm((9 * cb, nz * cb2), BF16),
            vm((2, 9 * cb, nz * hrows), BF16),
            vm((2, 9 * cb, cells), F32),
            vm((9 * cb, cells), F32),
            vm((3, 9 * cb, cells), F32),
            vm((nz, cb2, cells), BF16),
            vm((2, nz, hrows, cells), BF16),
            vm((n * piece, full), F32),
            *reduce_bufs,
            *reduce_bufs,
            dma((nz,)), dma((nz,)), dma((2, nz)), dma((2, nz)),
            dma((nz,)), dma((nz,)), dma((2,)), dma((2,)),
            dma((nz,)), dma((nz,)), dma((2, nz)), dma((2, nz)),
            dma((n,)), dma((n,)), dma((n,)), dma((n,)),
            dma((n,)), dma((n,)), dma((n,)), dma((n,)),
        ],
        compiler_params=pltpu.CompilerParams(
            collective_id=0, has_side_effects=True, vmem_limit_bytes=48 << 20
        ),
    )(block, mask.reshape(ys, -1),
      pltpu.with_memory_space_constraint(w_first, pltpu.HBM),
      pltpu.with_memory_space_constraint(w_second, pltpu.HBM))
    return (
        gf.reshape(cb, 1, ys, zs),
        g1.reshape(taps, cb, full).transpose(0, 2, 1),
        g2.reshape(taps, cb, full).transpose(0, 2, 1),
    )


def solution(mesh):
    in_specs = (
        P("chan", "space", None, None),
        P("chan", "space", None, None),
        P("space", None, "chan"),
        P(),
        P(),
    )
    out_specs = (P("chan", "space", None, None), P(None, None, "chan"), P(None, None, "chan"))
    sizes = (mesh.shape["space"], mesh.shape["chan"])
    return jax.shard_map(
        functools.partial(body, *sizes),
        mesh=mesh, in_specs=in_specs, out_specs=out_specs, check_vma=False,
    )
```
